32 devices in a mesh: section: 4 (over y, core), shard: 2 (over x), tensor: 4 (over z).
Axes of the slice: x: 2, y: 2, z: 4, core: 2. Of those that a mesh axis runs over, the one named last changes fastest.
Arguments:
- gradient: bfloat16 [48, 2560, 1024], P('section', ('shard', 'tensor')), may hold values from -15000 to 15000
- momentum: float32 [48, 2560, 1024], P('section', ('shard', 'tensor')), may hold values from -28000 to 28000
- weight: bfloat16 [48, 2560, 1024], P('section', ('shard', 'tensor')), may hold values from -0.1875 to 0.1875
Outputs:
- new_weight: bfloat16 [48, 2560, 1024], P('section', ('shard', 'tensor'))
- new_momentum: float32 [48, 2560, 1024], P('section', ('shard', 'tensor'))
- update: bfloat16 [48, 2560, 1024], P('section', ('shard', 'tensor'))
The draws below stay inside these ranges and needn't reach their ends.
All inputs are finite; a program needn't handle non-finite values.
Results may differ from the reference program's by a relative error of at most 0.029.
Values may be sent and summed in bfloat16 or wider, within the bound.
A program may use at most 256 MiB of HBM per device.

```python
import math
import jax
import jax.numpy as jnp
from jax import lax

D = 1024
HID = 2560
ITERS = 3
GROUPS = 48
N_SHARD = 2
N_TENSOR = 4


def row_factors(top_log):
    band = HID // (N_SHARD * N_TENSOR)
    rows = jnp.arange(HID, dtype=jnp.int32)
    row_set = rows // band % N_TENSOR
    level = row_set.astype(jnp.float32) / max(N_TENSOR - 1, 1)
    return jnp.exp(level * top_log).reshape(1, HID, 1)


def scaled_field(key, gain):
    keys = jax.random.split(key, 3)
    shape = (GROUPS, HID, D)
    base = jnp.clip(jax.random.normal(keys[0], shape, jnp.float32), -4.0, 4.0)
    top = math.log(10.0)
    rise = row_factors(math.log(10.0))
    row_scale = jnp.exp(jax.random.uniform(keys[1], (GROUPS, HID, 1), jnp.float32, 0.0, top))
    col_scale = jnp.exp(jax.random.uniform(keys[2], (GROUPS, 1, D), jnp.float32, 0.0, math.log(10.0)))
    return (gain * base * row_scale * col_scale * rise).astype(jnp.float32)


def draw_gradient(key, part):
    return scaled_field(jax.random.fold_in(key, 11), 1.0).astype(jnp.bfloat16)


def draw_momentum(key, part):
    return scaled_field(jax.random.fold_in(key, 23), 2.0)


def steps_of(rng, dims, shards, least, top_value):
    def one(position, blocks):
        draws = jax.random.uniform(jax.random.fold_in(jax.random.fold_in(rng, 6), position), (blocks,), jnp.float32, least / len(shards), top_value / len(shards))
        return jnp.repeat(jnp.exp(draws), dims[position] // blocks).reshape((-1,) + (1,) * (len(dims) - position - 1))

    loudness = one(*shards[0])
    for cut in shards[1:]:
        loudness = loudness * one(*cut)
    return loudness


def normal_values(own_key, dims, width, bound, cuts=(), held_as=jnp.bfloat16):
    entries = jax.random.normal(own_key, dims, jnp.float32) * width
    if len(cuts) > 0:
        entries = steps_of(own_key, dims, cuts, -0.22, 0.18) * entries
    return jnp.clip(entries, min=-bound, max=bound).astype(held_as)


def setup_inputs(seed: int = 0) -> dict:
    splits = jax.random.split(jax.random.key(seed), 4)
    return {
        "gradient": draw_gradient(jax.random.fold_in(splits[3], 71), 0),
        "momentum": draw_momentum(jax.random.fold_in(splits[3], 71), 0),
        "weight": normal_values(splits[2], (GROUPS, HID, D), D ** -0.5, 0.1875, ((0, 4), (1, 8))),
    }


decay_rate = 0.95
epsilon = 1e-07
coeff_one = 3.4445
coeff_two = -4.775
coeff_three = 2.0315
learn_rate = 0.02
weight_decay = 0.1

def orthogonalize(nesterov):
    values = nesterov.astype(jnp.float32)
    current = (values / (jnp.sqrt(jnp.sum(values * values)) + epsilon)).astype(jnp.bfloat16)
    band = HID // (N_SHARD * N_TENSOR)
    for iteration in range(ITERS):
        blocks = current.astype(jnp.float32).reshape(N_SHARD, N_TENSOR, band, D)
        partial_value = jnp.einsum('strd,stre->tde', blocks, blocks)
        rounded = lax.optimization_barrier(partial_value.astype(jnp.bfloat16))
        gram = lax.optimization_barrier(jnp.sum(rounded.astype(jnp.float32), axis=0))
        gram_bf = gram.astype(jnp.bfloat16)
        squared = jnp.dot(gram_bf, gram_bf, preferred_element_type=jnp.float32)
        mixer = (coeff_two * gram + coeff_three * squared).astype(jnp.bfloat16)
        mixed = jnp.dot(current, mixer, preferred_element_type=jnp.float32)
        current = (coeff_one * current.astype(jnp.float32) + mixed).astype(jnp.bfloat16)
    update_gain = 0.2 * math.sqrt(max(HID, D))
    return (update_gain * current.astype(jnp.float32)).astype(jnp.bfloat16)

def one_matrix(items):
    gradient, momentum, weight = items
    grad_values = gradient.astype(jnp.float32)
    new_momentum = decay_rate * momentum + grad_values
    nesterov = (grad_values + decay_rate * new_momentum).astype(jnp.bfloat16)
    update = orthogonalize(nesterov)
    weight_values = weight.astype(jnp.float32)
    new_weight = (weight_values - learn_rate * (update.astype(jnp.float32) + weight_decay * weight_values)).astype(jnp.bfloat16)
    return (new_weight, new_momentum, update)

def reference(gradient, momentum, weight):
    new_weight, new_momentum, update = lax.map(one_matrix, (gradient, momentum, weight))
    return (new_weight, new_momentum, update)
```

```python
import math

import jax
import jax.numpy as jnp
from jax import lax
from jax.experimental import pallas as pl
from jax.experimental.pallas import tpu as pltpu
from jax.sharding import PartitionSpec as P

ITERS = 3
BLK = 256
CHUNK = 1

decay_rate = 0.95
epsilon = 1e-07
coeff_one = 3.4445
coeff_two = -4.775
coeff_three = 2.0315
learn_rate = 0.02
weight_decay = 0.1


def pieces(width):
    nb = width // BLK
    half = BLK // 2
    out = []
    for i in range(nb):
        for j in range(i, nb):
            for h in range(2):
                if i == 0:
                    row, col = h * half, j * BLK
                elif 2 * i < nb:
                    row, col = i * BLK + h * half, (j - i) * BLK
                elif 2 * i > nb:
                    row, col = (nb - i) * BLK + h * half, j * BLK
                else:
                    row, col = i * BLK, (j - i) * BLK + h * (width // 2)
                out.append((i, j, h, row, col))
    return out


def packed_rows(width):
    return (width // BLK // 2) * BLK + BLK // 2


def gram_kernel(*refs):
    inputs, out_ref = refs[:-1], refs[-1]
    width = out_ref.shape[2]
    nb = width // BLK
    half = BLK // 2
    contract = (((0,), (0,)), ((), ()))
    for i in range(nb):
        value = None
        for ref in inputs:
            term = lax.dot_general(
                ref[0, :, pl.ds(i * BLK, BLK)],
                ref[0, :, pl.ds(i * BLK, width - i * BLK)],
                contract,
                preferred_element_type=jnp.float32,
            )
            value = term if value is None else value + term
        value = value.astype(jnp.bfloat16)
        for bi, bj, h, row, col in pieces(width):
            if bi == i:
                out_ref[0, pl.ds(row, half), pl.ds(col, BLK)] = value[
                    h * half : (h + 1) * half, (bj - i) * BLK : (bj - i + 1) * BLK
                ]


def gram_packed(*inputs):
    count, width = inputs[0].shape[0], inputs[0].shape[2]
    rows = packed_rows(width)
    depth = sum(x.shape[1] for x in inputs)
    return pl.pallas_call(
        gram_kernel,
        grid=(count,),
        in_specs=[pl.BlockSpec((1,) + x.shape[1:], lambda k: (k, 0, 0)) for x in inputs],
        out_specs=pl.BlockSpec((1, rows, width), lambda k: (k, 0, 0)),
        out_shape=jax.ShapeDtypeStruct((count, rows, width), jnp.bfloat16),
        compiler_params=pltpu.CompilerParams(vmem_limit_bytes=32 << 20),
        cost_estimate=pl.CostEstimate(
            flops=count * 2 * depth * width**2,
            bytes_accessed=count * 2 * (depth + rows) * width,
            transcendentals=0,
        ),
    )(*inputs)


def newton_kernel(gain, packed_ref, inputs, outputs, gram, total, gram_b, mix_b, total_b, holder):
    width = gram.shape[0]
    nb = width // BLK
    half = BLK // 2

    def blk(i):
        return pl.ds(i * BLK, BLK)

    trace = jnp.zeros((1, 1), jnp.float32)
    row_id = lax.broadcasted_iota(jnp.int32, (half, BLK), 0)
    col_id = lax.broadcasted_iota(jnp.int32, (half, BLK), 1)
    for i, j, h, row, col in pieces(width):
        if i == j:
            part = packed_ref[0, pl.ds(row, half), pl.ds(col, BLK)].astype(jnp.float32)
            part = jnp.where(row_id + h * half == col_id, part, 0.0)
            trace = trace + jnp.sum(jnp.sum(part, axis=1, keepdims=True), axis=0, keepdims=True)
    inverse = 1.0 / (jnp.sqrt(trace) + epsilon)
    for i, j, h, row, col in pieces(width):
        part = packed_ref[0, pl.ds(row, half), pl.ds(col, BLK)].astype(jnp.float32)
        gram[pl.ds(i * BLK + h * half, half), blk(j)] = part * inverse * inverse
    for i in range(nb):
        for j in range(i, nb):
            value = gram[blk(i), blk(j)]
            gram_b[blk(i), blk(j)] = value.astype(jnp.bfloat16)
            if j > i:
                gram_b[blk(j), blk(i)] = value.T.astype(jnp.bfloat16)

    def product(left, right, finish, full=None, keep=None):
        for i in range(nb):
            cols = pl.ds(i * BLK, width - i * BLK)
            value = jnp.dot(left[blk(i), :], right[:, cols], preferred_element_type=jnp.float32)
            value = finish(blk(i), cols, value)
            if keep is not None:
                keep[blk(i), cols] = value
            if full is not None:
                full[blk(i), cols] = value.astype(jnp.bfloat16)
                for j in range(i + 1, nb):
                    part = value[:, (j - i) * BLK : (j - i + 1) * BLK]
                    full[blk(j), blk(i)] = part.T.astype(jnp.bfloat16)

    def step_of(step, lead):
        product(
            gram_b,
            gram_b,
            lambda r, c, v: coeff_two * gram[r, c] + coeff_three * v,
            full=mix_b,
        )

        @pl.when(step == 0)
        def _():
            for i in range(nb):
                cols = pl.ds(i * BLK, width - i * BLK)
                total[blk(i), cols] = mix_b[blk(i), cols].astype(jnp.float32)
            total_b[...] = mix_b[...]

        @pl.when(step > 0)
        def _():
            def join(r, c, v):
                return coeff_one * total[r, c] + lead * mix_b[r, c].astype(jnp.float32) + v

            product(total_b, mix_b, join, keep=total, full=holder)
            total_b[...] = holder[...]

        @pl.when(step < ITERS - 1)
        def _():
            product(
                gram_b,
                mix_b,
                lambda r, c, v: coeff_one * gram[r, c] + v,
                full=holder,
                keep=gram,
            )
            product(
                mix_b,
                holder,
                lambda r, c, v: coeff_one * gram[r, c] + v,
                full=gram_b,
                keep=gram,
            )

        return lead * coeff_one

    lax.fori_loop(0, ITERS, step_of, jnp.float32(1.0))
    scale = inverse * gain
    for i in range(nb):
        for j in range(i, nb):
            value = total[blk(i), blk(j)]
            if i == j:
                r = lax.broadcasted_iota(jnp.int32, (BLK, BLK), 0)
                c = lax.broadcasted_iota(jnp.int32, (BLK, BLK), 1)
                value = value + jnp.where(r == c, coeff_one**ITERS, 0.0)
            value = value * scale
            holder[blk(i), blk(j)] = value.astype(jnp.bfloat16)
            if j > i:
                holder[blk(j), blk(i)] = value.T.astype(jnp.bfloat16)


    for x, out in zip(inputs, outputs):
        out[0] = jnp.dot(x[0], holder[...], preferred_element_type=jnp.float32).astype(
            jnp.bfloat16
        )


def updates(packed, gain, *inputs):
    count, rows, width = packed.shape
    parts = len(inputs)
    depth = sum(x.shape[1] for x in inputs)

    def kernel(packed_ref, *refs):
        newton_kernel(gain, packed_ref, refs[:parts], refs[parts : 2 * parts], *refs[2 * parts :])

    specs = [pl.BlockSpec((1,) + x.shape[1:], lambda k: (k, 0, 0)) for x in inputs]
    return pl.pallas_call(
        kernel,
        grid=(count,),
        in_specs=[pl.BlockSpec((1, rows, width), lambda k: (k, 0, 0))] + specs,
        out_specs=specs,
        out_shape=[jax.ShapeDtypeStruct(x.shape, jnp.bfloat16) for x in inputs],
        scratch_shapes=[pltpu.VMEM((width, width), jnp.float32)] * 2
        + [pltpu.VMEM((width, width), jnp.bfloat16)] * 4,
        compiler_params=pltpu.CompilerParams(vmem_limit_bytes=48 << 20),
        cost_estimate=pl.CostEstimate(
            flops=count * (12 * width**3 + 2 * depth * width**2),
            bytes_accessed=count * (2 * rows + 4 * depth) * width,
            transcendentals=0,
        ),
    )(packed, *inputs)


def gram_sum(packed):
    if lax.axis_size("tensor") != 4:
        return lax.psum(packed, "tensor")

    def added(x, y):
        return (x.astype(jnp.float32) + y.astype(jnp.float32)).astype(jnp.bfloat16)

    place = lax.axis_index("tensor")
    inner = added(packed, lax.ppermute(packed, "tensor", [(0, 1), (3, 2)]))
    whole = added(inner, lax.ppermute(inner, "tensor", [(1, 2), (2, 1)]))
    handed = lax.ppermute(whole, "tensor", [(1, 0), (2, 3)])
    return jnp.where((place == 1) | (place == 2), whole, handed)


def pad_slots(values, padded_count):
    extra = padded_count - values.shape[0]
    if extra == 0:
        return values
    filler = jnp.zeros((extra,) + values.shape[1:], values.dtype)
    return jnp.concatenate([values, filler], axis=0)


def update_pairs(nesterov, gain):
    half = nesterov.shape[0] // 2
    me = lax.axis_index("shard")
    swap = [(0, 1), (1, 0)]
    own, back = [], []
    for start in range(0, half, CHUNK):
        size = min(CHUNK, half - start)
        kept = lax.dynamic_slice_in_dim(nesterov, me * half + start, size, 0)
        sent = lax.dynamic_slice_in_dim(nesterov, (1 - me) * half + start, size, 0)
        got = lax.ppermute(sent, "shard", swap)
        packed = gram_sum(gram_packed(kept, got))
        mine, theirs = updates(packed, gain, kept, got)
        back.append(lax.ppermute(theirs, "shard", swap))
        own.append(mine)
    first = jnp.concatenate(own + back, axis=0)
    second = jnp.concatenate(back + own, axis=0)
    return jnp.where(me == 0, first, second)


def update_dealt(nesterov, shards, gain):
    count = nesterov.shape[0]
    slots = (count + shards - 1) // shards
    dealt = lax.all_to_all(
        pad_slots(nesterov, slots * shards), "shard", split_axis=0, concat_axis=1, tiled=True
    )
    (turned,) = updates(gram_sum(gram_packed(dealt)), gain, dealt)
    update = lax.all_to_all(turned, "shard", split_axis=1, concat_axis=0, tiled=True)
    return update[:count]


def local(gradient, momentum, weight):
    shards = lax.axis_size("shard")
    hidden = gradient.shape[1] * shards * lax.axis_size("tensor")
    gain = 0.2 * math.sqrt(max(hidden, gradient.shape[2]))
    grad_values = gradient.astype(jnp.float32)
    new_momentum = decay_rate * momentum + grad_values
    nesterov = (grad_values + decay_rate * new_momentum).astype(jnp.bfloat16)
    if shards == 2 and gradient.shape[0] % 2 == 0:
        update = update_pairs(nesterov, gain)
    else:
        update = update_dealt(nesterov, shards, gain)
    weight_values = weight.astype(jnp.float32)
    new_weight = (
        weight_values - learn_rate * (update.astype(jnp.float32) + weight_decay * weight_values)
    ).astype(jnp.bfloat16)
    return (new_weight, new_momentum, update)


def solution(mesh):
    spec = P("section", ("shard", "tensor"), None)
    return jax.shard_map(
        local,
        mesh=mesh,
        in_specs=(spec, spec, spec),
        out_specs=(spec, spec, spec),
        check_vma=False,
    )
```

```python
import math

import jax
import jax.numpy as jnp
from jax import lax
from jax.experimental import pallas as pl
from jax.experimental.pallas import tpu as pltpu
from jax.sharding import PartitionSpec as P

ITERS = 3
BLK = 256

decay_rate = 0.95
epsilon = 1e-07
coeff_one = 3.4445
coeff_two = -4.775
coeff_three = 2.0315
learn_rate = 0.02
weight_decay = 0.1


def pieces(width):
    nb = width // BLK
    half = BLK // 2
    out = []
    for i in range(nb):
        for j in range(i, nb):
            for h in range(2):
                if i == 0:
                    row, col = h * half, j * BLK
                elif 2 * i < nb:
                    row, col = i * BLK + h * half, (j - i) * BLK
                elif 2 * i > nb:
                    row, col = (nb - i) * BLK + h * half, j * BLK
                else:
                    row, col = i * BLK, (j - i) * BLK + h * (width // 2)
                out.append((i, j, h, row, col))
    return out


def packed_rows(width):
    return (width // BLK // 2) * BLK + BLK // 2


def gram_kernel(*refs):
    inputs, out_ref = refs[:-1], refs[-1]
    width = out_ref.shape[2]
    nb = width // BLK
    half = BLK // 2
    contract = (((0,), (0,)), ((), ()))
    for i in range(nb):
        value = None
        for ref in inputs:
            term = lax.dot_general(
                ref[0, :, pl.ds(i * BLK, BLK)],
                ref[0, :, pl.ds(i * BLK, width - i * BLK)],
                contract,
                preferred_element_type=jnp.float32,
            )
            value = term if value is None else value + term
        value = value.astype(jnp.bfloat16)
        for bi, bj, h, row, col in pieces(width):
            if bi == i:
                out_ref[0, pl.ds(row, half), pl.ds(col, BLK)] = value[
                    h * half : (h + 1) * half, (bj - i) * BLK : (bj - i + 1) * BLK
                ]


def gram_packed(*inputs):
    count, width = inputs[0].shape[0], inputs[0].shape[2]
    rows = packed_rows(width)
    depth = sum(x.shape[1] for x in inputs)
    return pl.pallas_call(
        gram_kernel,
        grid=(count,),
        in_specs=[pl.BlockSpec((1,) + x.shape[1:], lambda k: (k, 0, 0)) for x in inputs],
        out_specs=pl.BlockSpec((1, rows, width), lambda k: (k, 0, 0)),
        out_shape=jax.ShapeDtypeStruct((count, rows, width), jnp.bfloat16),
        compiler_params=pltpu.CompilerParams(vmem_limit_bytes=32 << 20),
        cost_estimate=pl.CostEstimate(
            flops=count * 2 * depth * width**2,
            bytes_accessed=count * 2 * (depth + rows) * width,
            transcendentals=0,
        ),
    )(*inputs)


def newton_kernel(gain, packed_ref, inputs, outputs, gram, total, gram_b, mix_b, total_b, holder):
    width = gram.shape[0]
    nb = width // BLK
    half = BLK // 2

    def blk(i):
        return pl.ds(i * BLK, BLK)

    trace = jnp.zeros((1, 1), jnp.float32)
    row_id = lax.broadcasted_iota(jnp.int32, (half, BLK), 0)
    col_id = lax.broadcasted_iota(jnp.int32, (half, BLK), 1)
    for i, j, h, row, col in pieces(width):
        if i == j:
            part = packed_ref[0, pl.ds(row, half), pl.ds(col, BLK)].astype(jnp.float32)
            part = jnp.where(row_id + h * half == col_id, part, 0.0)
            trace = trace + jnp.sum(jnp.sum(part, axis=1, keepdims=True), axis=0, keepdims=True)
    inverse = 1.0 / (jnp.sqrt(trace) + epsilon)
    for i, j, h, row, col in pieces(width):
        part = packed_ref[0, pl.ds(row, half), pl.ds(col, BLK)].astype(jnp.float32)
        gram[pl.ds(i * BLK + h * half, half), blk(j)] = part * inverse * inverse
    for i in range(nb):
        for j in range(i, nb):
            value = gram[blk(i), blk(j)]
            gram_b[blk(i), blk(j)] = value.astype(jnp.bfloat16)
            if j > i:
                gram_b[blk(j), blk(i)] = value.T.astype(jnp.bfloat16)

    def product(left, right, finish, full=None, keep=None):
        for i in range(nb):
            cols = pl.ds(i * BLK, width - i * BLK)
            value = jnp.dot(left[blk(i), :], right[:, cols], preferred_element_type=jnp.float32)
            value = finish(blk(i), cols, value)
            if keep is not None:
                keep[blk(i), cols] = value
            if full is not None:
                full[blk(i), cols] = value.astype(jnp.bfloat16)
                for j in range(i + 1, nb):
                    part = value[:, (j - i) * BLK : (j - i + 1) * BLK]
                    full[blk(j), blk(i)] = part.T.astype(jnp.bfloat16)

    def step_of(step, lead):
        product(
            gram_b,
            gram_b,
            lambda r, c, v: coeff_two * gram[r, c] + coeff_three * v,
            full=mix_b,
        )

        @pl.when(step == 0)
        def _():
            for i in range(nb):
                cols = pl.ds(i * BLK, width - i * BLK)
                total[blk(i), cols] = mix_b[blk(i), cols].astype(jnp.float32)
            total_b[...] = mix_b[...]

        @pl.when(step > 0)
        def _():
            def join(r, c, v):
                return coeff_one * total[r, c] + lead * mix_b[r, c].astype(jnp.float32) + v

            product(total_b, mix_b, join, keep=total, full=holder)
            total_b[...] = holder[...]

        @pl.when(step < ITERS - 1)
        def _():
            product(
                gram_b,
                mix_b,
                lambda r, c, v: coeff_one * gram[r, c] + v,
                full=holder,
                keep=gram,
            )
            product(
                mix_b,
                holder,
                lambda r, c, v: coeff_one * gram[r, c] + v,
                full=gram_b,
                keep=gram,
            )

        return lead * coeff_one

    lax.fori_loop(0, ITERS, step_of, jnp.float32(1.0))
    scale = inverse * gain
    for i in range(nb):
        for j in range(i, nb):
            value = total[blk(i), blk(j)]
            if i == j:
                r = lax.broadcasted_iota(jnp.int32, (BLK, BLK), 0)
                c = lax.broadcasted_iota(jnp.int32, (BLK, BLK), 1)
                value = value + jnp.where(r == c, coeff_one**ITERS, 0.0)
            value = value * scale
            holder[blk(i), blk(j)] = value.astype(jnp.bfloat16)
            if j > i:
                holder[blk(j), blk(i)] = value.T.astype(jnp.bfloat16)


    for x, out in zip(inputs, outputs):
        out[0] = jnp.dot(x[0], holder[...], preferred_element_type=jnp.float32).astype(
            jnp.bfloat16
        )


def updates(packed, gain, *inputs):
    count, rows, width = packed.shape
    parts = len(inputs)
    depth = sum(x.shape[1] for x in inputs)

    def kernel(packed_ref, *refs):
        newton_kernel(gain, packed_ref, refs[:parts], refs[parts : 2 * parts], *refs[2 * parts :])

    specs = [pl.BlockSpec((1,) + x.shape[1:], lambda k: (k, 0, 0)) for x in inputs]
    return pl.pallas_call(
        kernel,
        grid=(count,),
        in_specs=[pl.BlockSpec((1, rows, width), lambda k: (k, 0, 0))] + specs,
        out_specs=specs,
        out_shape=[jax.ShapeDtypeStruct(x.shape, jnp.bfloat16) for x in inputs],
        scratch_shapes=[pltpu.VMEM((width, width), jnp.float32)] * 2
        + [pltpu.VMEM((width, width), jnp.bfloat16)] * 4,
        compiler_params=pltpu.CompilerParams(vmem_limit_bytes=48 << 20),
        cost_estimate=pl.CostEstimate(
            flops=count * (12 * width**3 + 2 * depth * width**2),
            bytes_accessed=count * (2 * rows + 4 * depth) * width,
            transcendentals=0,
        ),
    )(packed, *inputs)


def pad_slots(values, padded_count):
    extra = padded_count - values.shape[0]
    if extra == 0:
        return values
    filler = jnp.zeros((extra,) + values.shape[1:], values.dtype)
    return jnp.concatenate([values, filler], axis=0)


def added(x, y):
    return (x.astype(jnp.float32) + y.astype(jnp.float32)).astype(jnp.bfloat16)


def new_weights(weight, update):
    values = weight.astype(jnp.float32)
    return (
        values - learn_rate * (update.astype(jnp.float32) + weight_decay * values)
    ).astype(jnp.bfloat16)


def steps_in_line(nesterov, weight, gain):
    half = nesterov.shape[0] // 2
    me = lax.axis_index("shard")
    place = lax.axis_index("tensor")
    central = (place == 1) | (place == 2)
    swap = [(0, 1), (1, 0)]

    def trade(k):
        kept = lax.dynamic_slice_in_dim(nesterov, me * half + k, 1, 0)
        sent = lax.dynamic_slice_in_dim(nesterov, (1 - me) * half + k, 1, 0)
        return kept, lax.ppermute(sent, "shard", swap)

    pairs = [trade(k) for k in range(half)]
    update, changed = jnp.zeros_like(weight), jnp.zeros_like(weight)

    def put(held, k, value):
        update, changed = held
        old = lax.dynamic_slice_in_dim(weight, k, 1, 0)
        return (
            lax.dynamic_update_slice_in_dim(update, value, k, 0),
            lax.dynamic_update_slice_in_dim(changed, new_weights(old, value), k, 0),
        )

    held = (update, changed)
    packed, inner, whole = {}, {}, {}
    from_a, from_b, from_c, returned = {}, {}, {}, {}
    gate = None
    for tick in range(half + 3):
        a, b, c, n = tick, tick - 1, tick - 2, tick - 3
        if gate is not None:
            live = [x[k] for x, k in ((from_a, b), (from_b, c), (from_c, n)) if 0 <= k < half]
            gate, *live = lax.optimization_barrier((gate, *live))
            for x, k in ((from_a, b), (from_b, c), (from_c, n)):
                if 0 <= k < half:
                    x[k] = live.pop(0)
        sends = {}
        if a < half:
            sends["a"] = packed[a] = gram_packed(*pairs[a])
        if 0 <= b < half:
            sends["b"] = inner[b] = added(packed[b], from_a[b])
        if 0 <= c < half:
            sends["c"] = whole[c] = added(inner[c], from_b[c])
        if n >= 0:
            sends["n"] = jnp.where(central, whole[n], from_c[n])
            sends = lax.optimization_barrier(sends)
        if a < half:
            packed[a] = sends["a"]
            from_a[a] = lax.ppermute(sends["a"], "tensor", [(0, 1), (3, 2)])
        if 0 <= b < half:
            inner[b] = sends["b"]
            from_b[b] = lax.ppermute(sends["b"], "tensor", [(1, 2), (2, 1)])
        if 0 <= c < half:
            whole[c] = sends["c"]
            from_c[c] = lax.ppermute(sends["c"], "tensor", [(1, 0), (2, 3)])
        if n >= 0:
            mine, theirs = updates(sends["n"], gain, *pairs[n])
            gate = theirs
            returned[n] = lax.ppermute(theirs, "shard", swap)
            held = put(held, me * half + n, mine)
    for n in range(half):
        held = put(held, (1 - me) * half + n, returned[n])
    return held


def update_dealt(nesterov, shards, gain):
    count = nesterov.shape[0]
    slots = (count + shards - 1) // shards
    dealt = lax.all_to_all(
        pad_slots(nesterov, slots * shards), "shard", split_axis=0, concat_axis=1, tiled=True
    )
    (turned,) = updates(lax.psum(gram_packed(dealt), "tensor"), gain, dealt)
    update = lax.all_to_all(turned, "shard", split_axis=1, concat_axis=0, tiled=True)
    return update[:count]


def local(gradient, momentum, weight):
    shards = lax.axis_size("shard")
    hidden = gradient.shape[1] * shards * lax.axis_size("tensor")
    gain = 0.2 * math.sqrt(max(hidden, gradient.shape[2]))
    grad_values = gradient.astype(jnp.float32)
    new_momentum = decay_rate * momentum + grad_values
    nesterov = (grad_values + decay_rate * new_momentum).astype(jnp.bfloat16)
    count = gradient.shape[0]
    if shards == 2 and count % 2 == 0 and lax.axis_size("tensor") == 4:
        update, new_weight = steps_in_line(nesterov, weight, gain)
    else:
        update = update_dealt(nesterov, shards, gain)
        new_weight = new_weights(weight, update)
    return (new_weight, new_momentum, update)


def solution(mesh):
    spec = P("section", ("shard", "tensor"), None)
    return jax.shard_map(
        local,
        mesh=mesh,
        in_specs=(spec, spec, spec),
        out_specs=(spec, spec, spec),
        check_vma=False,
    )
```
